256 devices in a mesh: rows: 16 (over x, y_lo, core), cols: 16 (over z, y_hi).
Axes of the slice: x: 4, y: 4 (y_hi: 2, y_lo: 2; y = y_hi * 2 + y_lo), z: 8, core: 2. Of those that a mesh axis runs over, the one named last changes fastest.
Arguments:
- unary: float32 [21, 256, 2048], P(None, 'rows', 'cols'), may hold values from -8 to 300
- features: bfloat16 [64, 256, 2048], P(None, 'rows', 'cols'), may hold values from -9 to 9
- compat: float32 [21, 21], replicated, may hold values from -6 to 6
- grad_output: float32 [21, 256, 2048], P(None, 'rows', 'cols'), may hold values from -6 to 6
Outputs:
- unary_grad: float32 [21, 256, 2048], P(None, 'rows', 'cols')
- feature_grad: float32 [64, 256, 2048], P(None, 'rows', 'cols')
- compat_grad: float32 [21, 21], replicated
The draws below stay inside these ranges and needn't reach their ends.
All inputs are finite; a program needn't handle non-finite values.
Results may differ from the reference program's by a relative error of at most 0.0003.
Values may be sent and summed in bfloat16 or wider, within the bound.
A program may use at most 128 MiB of HBM per device.

```python
import math
import jax
import jax.numpy as jnp
from jax import lax

CLASSES = 21
FEAT = 64
ITERS = 2
NH = 256
NW = 2048


def draw_unary(key, part):
    base_key = jax.random.fold_in(key, 0)
    return jnp.clip(2.0 * jax.random.normal(base_key, (CLASSES, NH, NW), jnp.float32), -8.0, 8.0)


def block_levels(stream_key, shape, pieces, low, top_value):
    def one(axis_at, parts):
        heights = jax.random.uniform(jax.random.fold_in(jax.random.fold_in(stream_key, 6), axis_at), (parts,), jnp.float32, low / len(pieces), top_value / len(pieces))
        return jnp.repeat(jnp.exp(heights), shape[axis_at] // parts).reshape((-1,) + (1,) * (len(shape) - axis_at - 1))

    gain = one(*pieces[0])
    for cut in pieces[1:]:
        gain = gain * one(*cut)
    return gain


def gaussian(own_key, shape, deviation, most, pieces=(), held_as=jnp.bfloat16):
    array = deviation * jax.random.normal(own_key, shape, jnp.float32)
    if pieces:
        array = array * block_levels(own_key, shape, pieces, -0.22, 0.18)
    return jnp.clip(array, -most, most).astype(held_as)


def setup_inputs(seed: int = 0) -> dict:
    arg_keys = jax.random.split(jax.random.key(seed), 5)
    return {
        "unary": draw_unary(jax.random.fold_in(arg_keys[4], 71), 0),
        "features": gaussian(arg_keys[1], (FEAT, NH, NW), 1.5, 9.0, ((1, 16), (2, 16))),
        "compat": gaussian(arg_keys[2], (CLASSES, CLASSES), 1.0, 6.0, (), jnp.float32),
        "grad_output": gaussian(arg_keys[3], (CLASSES, NH, NW), 1.0, 6.0, ((1, 16), (2, 16)), jnp.float32),
    }


THETA_PIXELS = 3.0
WINDOW_OFFSETS = [(row_step, col_step) for row_step in range(-3, 4) for col_step in range(-3, 4) if row_step != 0 or col_step != 0]

def spatial_weight(row_step, col_step):
    return math.exp(-(row_step * row_step + col_step * col_step) / (2.0 * THETA_PIXELS * THETA_PIXELS))

def shifted_view(padded, row_step, col_step, height, width_cells):
    return padded[:, 3 + row_step:3 + row_step + height, 3 + col_step:3 + col_step + width_cells]

def affinity(padded_features):
    height = padded_features.shape[1] - 6
    width_cells = padded_features.shape[2] - 6
    center = shifted_view(padded_features, 0, 0, height, width_cells).astype(jnp.float32)
    factor = 1.0 / (2.0 * padded_features.shape[0])
    layers = []
    for row_step, col_step in WINDOW_OFFSETS:
        shifted = shifted_view(padded_features, row_step, col_step, height, width_cells).astype(jnp.float32)
        distance = lax.optimization_barrier(jnp.sum((shifted - center) * (shifted - center), axis=0))
        layers.append(spatial_weight(row_step, col_step) * jnp.exp(-distance * factor))
    return jnp.stack(layers)

def message(kernel, padded):
    height = kernel.shape[1]
    width_cells = kernel.shape[2]
    total = jnp.zeros((padded.shape[0], height, width_cells), jnp.float32)
    for number, (row_step, col_step) in enumerate(WINDOW_OFFSETS):
        total = total + kernel[number][None] * shifted_view(padded, row_step, col_step, height, width_cells)
    return total

def pair_terms(grad_padded, prob_padded):
    height = grad_padded.shape[1] - 6
    width_cells = grad_padded.shape[2] - 6
    grad_center = shifted_view(grad_padded, 0, 0, height, width_cells)
    prob_center = shifted_view(prob_padded, 0, 0, height, width_cells)
    layers = []
    for row_step, col_step in WINDOW_OFFSETS:
        prob_shift = shifted_view(prob_padded, row_step, col_step, height, width_cells)
        grad_shift = shifted_view(grad_padded, row_step, col_step, height, width_cells)
        layers.append(lax.optimization_barrier(jnp.sum(grad_center * prob_shift + grad_shift * prob_center, axis=0)))
    return jnp.stack(layers)

def feature_term(coefs, kernel, padded_features):
    height = kernel.shape[1]
    width_cells = kernel.shape[2]
    center = shifted_view(padded_features, 0, 0, height, width_cells).astype(jnp.float32)
    factor = 1.0 / padded_features.shape[0]
    total = jnp.zeros(center.shape, jnp.float32)
    for number, (row_step, col_step) in enumerate(WINDOW_OFFSETS):
        shifted = shifted_view(padded_features, row_step, col_step, height, width_cells).astype(jnp.float32)
        weight_map = coefs[number] * kernel[number] * factor
        total = total + weight_map[None] * (shifted - center)
    return total

def mix(compat, values):
    return jnp.einsum('cd,dhw->chw', compat, values, precision=lax.Precision.HIGHEST)

def mix_back(compat, values):
    return jnp.einsum('cd,chw->dhw', compat, values, precision=lax.Precision.HIGHEST)

def outer_sum(left, right):
    return jnp.einsum('chw,dhw->cd', left, right, precision=lax.Precision.HIGHEST)

def softmax_grad(prob, cotangent):
    return prob * (cotangent - lax.optimization_barrier(jnp.sum(cotangent * prob, axis=0, keepdims=True)))

def pad_three(values):
    return jnp.pad(values, ((0, 0), (3, 3), (3, 3)))

def reference(unary, features, compat, grad_output):
    feat_wide = pad_three(features)
    kernel = affinity(feat_wide)
    prob_list = [jax.nn.softmax(unary, axis=0)]
    message_list = []
    for step in range(ITERS):
        message_out = message(kernel, pad_three(prob_list[-1]))
        message_list.append(message_out)
        prob_list.append(jax.nn.softmax(unary - mix(compat, message_out), axis=0))
    cotangent = grad_output
    unary_sum = jnp.zeros(unary.shape, jnp.float32)
    compat_sum = jnp.zeros(compat.shape, jnp.float32)
    coefs = jnp.zeros((len(WINDOW_OFFSETS), unary.shape[1], unary.shape[2]), jnp.float32)
    for step in reversed(range(ITERS)):
        logit_grad = softmax_grad(prob_list[step + 1], cotangent)
        unary_sum = unary_sum + logit_grad
        compat_sum = compat_sum - outer_sum(logit_grad, message_list[step])
        msg_grad = -mix_back(compat, logit_grad)
        grad_wide = pad_three(msg_grad)
        cotangent = message(kernel, grad_wide)
        coefs = coefs + pair_terms(grad_wide, pad_three(prob_list[step]))
    unary_grad = unary_sum + softmax_grad(prob_list[0], cotangent)
    feature_grad = feature_term(coefs, kernel, feat_wide)
    compat_grad = compat_sum / math.sqrt(unary.shape[1] * unary.shape[2])
    return (unary_grad, feature_grad, compat_grad)
```

```python
import functools
import math

import jax
import jax.numpy as jnp
from jax import lax
from jax.experimental import pallas as pl
from jax.experimental.pallas import tpu as pltpu
from jax.sharding import PartitionSpec as P

REACH = 3
SPAN = 2 * REACH + 1
THETA_PIXELS = 3.0
MESH = pl.DeviceIdType.MESH
LANES = 128
TOP = 8
PLANE = 32
WIN = 24
F_GROUP = 16
PHASES = 4
HALF = 8

ROUTES = (
    (-1, 0, 1),
    (1, 0, 0),
    (0, -1, 3),
    (0, 1, 2),
    (-1, -1, 7),
    (-1, 1, 5),
    (1, -1, 6),
    (1, 1, 4),
)


def kernel(
    n_rows, n_cols, classes, feats,
    u_hbm, f_hbm, cm, g_hbm,
    ug_ref, fg_ref, cg_ref,
    u_v, g_v, f_v, f_plane, plane, f_shift, shift, kern, coef,
    prob, msg, lgrad,
    f_rows_f32, f_srow, f_rrow, f_sstrip, f_rstrip, f_strip,
    srow, rrow, sstrip, rstrip,
    ar_one, ar_two,
    in_sem, f_ssem, f_rsem, ssem, rsem, ar_ssem, ar_rsem,
):
    f32 = jnp.float32
    height = u_v.shape[1]
    r = lax.axis_index("rows")
    c = lax.axis_index("cols")
    lane = lax.broadcasted_iota(jnp.int32, (1, LANES), 1)
    lane_group = lane // 6
    from_left = (lane % 6) < 3

    loads = [
        pltpu.make_async_copy(f_hbm, f_v, in_sem.at[0]),
        pltpu.make_async_copy(u_hbm, u_v, in_sem.at[1]),
        pltpu.make_async_copy(g_hbm, g_v, in_sem.at[2]),
    ]
    for load in loads:
        load.start()

    def inside(dr, dc):
        ok = None
        for pos, step, size in ((r, dr, n_rows), (c, dc, n_cols)):
            if step:
                here = (pos > 0) if step < 0 else (pos < size - 1)
                ok = here if ok is None else jnp.logical_and(ok, here)
        return ok

    def target(dr, dc):
        return {"rows": r + dr, "cols": c + dc}

    @pl.when(r == 0)
    def _():
        f_rrow[0] = jnp.zeros_like(f_rrow[0])
        for k in range(PHASES):
            rrow[k, 0] = jnp.zeros_like(rrow[k, 0])
        for side in range(2):
            f_rstrip[side, 0] = jnp.zeros_like(f_rstrip[side, 0])
            for k in range(PHASES):
                rstrip[k, side, 0:HALF] = jnp.zeros((HALF, LANES), f32)

    @pl.when(r == n_rows - 1)
    def _():
        f_rrow[1] = jnp.zeros_like(f_rrow[1])
        for k in range(PHASES):
            rrow[k, 1] = jnp.zeros_like(rrow[k, 1])
        for side in range(2):
            f_rstrip[side, 2] = jnp.zeros_like(f_rstrip[side, 2])
            for k in range(PHASES):
                rstrip[k, side, PLANE - HALF:PLANE] = jnp.zeros((HALF, LANES), f32)

    for side, edge in ((0, 0), (1, n_cols - 1)):
        @pl.when(c == edge)
        def _(side=side):
            f_rstrip[side] = jnp.zeros_like(f_rstrip[side])
            for k in range(PHASES):
                rstrip[k, side] = jnp.zeros((PLANE, LANES), f32)

    barrier = pltpu.get_barrier_semaphore()
    for k in range(1, n_rows):
        pl.semaphore_signal(barrier, inc=1, device_id={"rows": lax.rem(r + k, n_rows), "cols": c}, device_id_type=MESH)
    for k in range(1, n_cols):
        pl.semaphore_signal(barrier, inc=1, device_id={"rows": r, "cols": lax.rem(c + k, n_cols)}, device_id_type=MESH)
    for dr, dc, _ in ROUTES[4:]:
        there = {"rows": lax.rem(r + dr + n_rows, n_rows), "cols": lax.rem(c + dc + n_cols, n_cols)}
        pl.semaphore_signal(barrier, inc=1, device_id=there, device_id_type=MESH)

    def pack_rows(source, count, base_row, dst):
        for ch in range(count):
            dst[3 * ch:3 * ch + 3, :] = source[ch, base_row:base_row + 3, :]

    loads[0].wait()
    f_plane[:, TOP:TOP + height, :] = f_v[...].astype(f32)
    for side, base_row in ((0, TOP), (1, TOP + height - 3)):
        pack_rows(f_plane, feats, base_row, f_rows_f32)
        f_srow[side] = f_rows_f32[...].astype(jnp.bfloat16)
    for group in range(feats // F_GROUP):
        tile = jnp.zeros((height, LANES), f32)
        for k in range(F_GROUP):
            turned = pltpu.roll(f_plane[group * F_GROUP + k, TOP:TOP + height, :], 6 * k + 3, 1)
            tile = jnp.where(lane_group == k, turned, tile)
        f_sstrip[group] = tile.astype(jnp.bfloat16)

    def softmax(values):
        top = jnp.max(values, axis=0, keepdims=True)
        grown = jnp.exp(values - top)
        return grown / jnp.sum(grown, axis=0, keepdims=True)

    def pack(k, ref):
        plane[:, TOP:TOP + height, :] = ref[...]
        tile = jnp.zeros((height, LANES), f32)
        for ch in range(classes):
            turned = pltpu.roll(ref[ch], (6 * ch + 3) % LANES, 1)
            tile = jnp.where(lane_group == ch, turned, tile)
        sstrip[k] = tile
        pack_rows(plane, classes, TOP, srow.at[k, 0])
        pack_rows(plane, classes, TOP + height - 3, srow.at[k, 1])

    def field_copy(k, way):
        dr, dc, slot = ROUTES[way]
        if dc == 0:
            src = srow.at[k, 0 if dr < 0 else 1]
            dst = rrow.at[k, slot]
        else:
            side = 1 if dc < 0 else 0
            if dr == 0:
                src = sstrip.at[k]
                dst = rstrip.at[k, side, pl.ds(HALF, height)]
            elif dr < 0:
                src = sstrip.at[k, pl.ds(0, HALF)]
                dst = rstrip.at[k, side, pl.ds(HALF + height, HALF)]
            else:
                src = sstrip.at[k, pl.ds(height - HALF, HALF)]
                dst = rstrip.at[k, side, pl.ds(0, HALF)]
        return pltpu.make_async_remote_copy(
            src_ref=src, dst_ref=dst, send_sem=ssem.at[k, way], recv_sem=rsem.at[k, way],
            device_id=target(dr, dc), device_id_type=MESH,
        )

    def feature_copy(way):
        dr, dc, slot = ROUTES[way]
        if dc == 0:
            src = f_srow.at[0 if dr < 0 else 1]
            dst = f_rrow.at[slot]
        else:
            src = f_sstrip
            dst = f_rstrip.at[1 if dc < 0 else 0, 1 - dr]
        return pltpu.make_async_remote_copy(
            src_ref=src, dst_ref=dst, send_sem=f_ssem.at[way], recv_sem=f_rsem.at[way],
            device_id=target(dr, dc), device_id_type=MESH,
        )

    def each_way(make, act):
        for way, (dr, dc, _) in enumerate(ROUTES):
            if act == "start":
                @pl.when(inside(dr, dc))
                def _(way=way):
                    make(way).start()
            elif act == "recv":
                @pl.when(inside(-dr, -dc))
                def _(way=way):
                    make(way).wait_recv()
            else:
                @pl.when(inside(dr, dc))
                def _(way=way):
                    make(way).wait_send()

    loads[1].wait()
    prob[0] = softmax(u_v[...])
    pack(0, prob.at[0])
    loads[2].wait()
    pl.semaphore_wait(barrier, n_rows - 1 + n_cols - 1 + 4)
    each_way(feature_copy, "start")
    each_way(functools.partial(field_copy, 0), "start")

    def turn(edge, own, dst, ch):
        for b in range(-REACH, REACH + 1):
            if b == 0:
                dst[b + REACH, ch] = own
            elif b > 0:
                dst[b + REACH, ch] = pltpu.roll(jnp.where(lane < b, edge, own), LANES - b, 1)
            else:
                dst[b + REACH, ch] = pltpu.roll(jnp.where(lane >= LANES + b, edge, own), -b, 1)

    each_way(feature_copy, "recv")
    for side, base_row in ((0, TOP - 3), (1, TOP + height)):
        f_rows_f32[...] = f_rrow[side].astype(f32)
        for ch in range(feats):
            f_plane[ch, base_row:base_row + 3, :] = f_rows_f32[3 * ch:3 * ch + 3, :]
    for group in range(feats // F_GROUP):
        for part in range(3):
            both = jnp.where(
                from_left, f_rstrip[0, part, group].astype(f32), f_rstrip[1, part, group].astype(f32)
            )
            f_strip[group, part * height:(part + 1) * height] = both
    for group in range(feats // F_GROUP):
        strip = f_strip[group, height - 3:height - 3 + WIN]

        def f_turn(k, carry, group=group):
            ch = group * F_GROUP + k
            edge = pltpu.roll(f_strip[group, height - 3:height - 3 + WIN], LANES - 3 - 6 * k, 1)
            turn(edge, f_plane[ch, TOP - 3:TOP - 3 + WIN, :], f_shift, ch)
            return carry

        lax.fori_loop(0, F_GROUP, f_turn, 0)

    factor = 1.0 / (2.0 * feats)
    spread = 1.0 / (2.0 * THETA_PIXELS * THETA_PIXELS)

    def rows_at(a):
        return slice(a, a + height)

    def affinity(bi, carry):
        def channels(i, acc):
            for extra in range(4):
                ch = 4 * i + extra
                center = f_shift[REACH, ch, rows_at(REACH), :]
                new = []
                for a in range(SPAN):
                    gap = f_shift[bi, ch, rows_at(a), :] - center
                    new.append(acc[a] + gap * gap)
                acc = tuple(new)
            return acc

        zero = jnp.zeros((height, LANES), f32)
        acc = lax.fori_loop(0, feats // 4, channels, (zero,) * SPAN)
        step = (bi - REACH).astype(f32)
        for a in range(SPAN):
            away = ((a - REACH) * (a - REACH) + step * step) * spread
            kern[bi * SPAN + a] = jnp.exp(-acc[a] * factor - away)
        return carry

    lax.fori_loop(0, SPAN, affinity, 0)
    kern[REACH * SPAN + REACH] = jnp.zeros((height, LANES), f32)

    def arrive(k):
        each_way(functools.partial(field_copy, k), "recv")
        for ch in range(classes):
            plane[ch, TOP - 3:TOP, :] = rrow[k, 0, 3 * ch:3 * ch + 3, :]
            plane[ch, TOP + height:TOP + height + 3, :] = rrow[k, 1, 3 * ch:3 * ch + 3, :]
        strip = jnp.where(from_left, rstrip[k, 0, TOP - 3:TOP - 3 + WIN], rstrip[k, 1, TOP - 3:TOP - 3 + WIN])

        def f_turn(i, carry):
            for extra in range(3):
                ch = 3 * i + extra
                edge = pltpu.roll(strip, LANES - 3 - 6 * ch, 1)
                turn(edge, plane[ch, TOP - 3:TOP - 3 + WIN, :], shift.at[k], ch)
            return carry

        lax.fori_loop(0, classes // 3, f_turn, 0)

    def spread_out(k, dst):
        for block in range(classes // 7):
            chans = slice(7 * block, 7 * block + 7)

            def step(bi, acc):
                for a in range(SPAN):
                    acc = acc + kern[bi * SPAN + a][None] * shift[k, bi, chans, rows_at(a), :]
                return acc

            dst[chans] = lax.fori_loop(0, SPAN, step, jnp.zeros((7, height, LANES), f32))

    def mix(transposed, source, finish):
        def one(ch, carry):
            acc = jnp.zeros((height, LANES), f32)
            for d in range(classes):
                weight = cm[d, ch] if transposed else cm[ch, d]
                acc = acc + weight * source[d]
            finish(ch, acc)
            return carry

        lax.fori_loop(0, classes, one, 0)

    def set_logits(t):
        def finish(ch, acc):
            prob[t, ch] = u_v[ch] - acc
        return finish

    def set_msg_grad(ch, acc):
        plane[ch, TOP:TOP + height, :] = -acc
        prob[PHASES - 1, ch] = -acc

    def softmax_grad(value, cotangent):
        return value * (cotangent - jnp.sum(cotangent * value, axis=0, keepdims=True))

    arrive(0)
    spread_out(0, msg.at[0])
    mix(False, msg.at[0], set_logits(1))
    prob[1] = softmax(prob[1])
    pack(1, prob.at[1])
    each_way(functools.partial(field_copy, 1), "start")
    arrive(1)
    spread_out(1, msg.at[1])
    mix(False, msg.at[1], set_logits(2))
    prob[2] = softmax(prob[2])

    lgrad[1] = softmax_grad(prob[2], g_v[...])
    mix(True, lgrad.at[1], set_msg_grad)
    pack(2, prob.at[PHASES - 1])
    each_way(functools.partial(field_copy, 2), "start")

    def by_pixel(ref):
        return jnp.concatenate([ref[:, y, :] for y in range(height)], axis=1)

    def outer(t):
        return lax.dot_general(
            by_pixel(lgrad.at[t]), by_pixel(msg.at[t]), (((1,), (1,)), ((), ())),
            precision=lax.Precision.HIGHEST, preferred_element_type=f32,
        )

    total = outer(1)
    arrive(2)
    spread_out(2, ug_ref)

    lgrad[0] = softmax_grad(prob[1], ug_ref[...])
    mix(True, lgrad.at[0], set_msg_grad)
    pack(3, prob.at[PHASES - 1])
    each_way(functools.partial(field_copy, 3), "start")

    pixels = height * n_rows * LANES * n_cols
    total = (total + outer(0)) * (-1.0 / math.sqrt(pixels))
    ar_one[r, 0:classes, 0:classes] = total

    def reduce_copy(stage, k):
        buf = (ar_one, ar_two)[stage]
        size, pos = ((n_rows, r), (n_cols, c))[stage]
        there = lax.rem(pos + k, size)
        device = {"rows": there, "cols": c} if stage == 0 else {"rows": r, "cols": there}
        return pltpu.make_async_remote_copy(
            src_ref=buf.at[pos], dst_ref=buf.at[pos],
            send_sem=ar_ssem.at[stage, k], recv_sem=ar_rsem.at[stage, pos],
            device_id=device, device_id_type=MESH,
        )

    def reduce_arrival(stage, k):
        buf = (ar_one, ar_two)[stage]
        size, pos = ((n_rows, r), (n_cols, c))[stage]
        there = lax.rem(pos + k, size)
        device = {"rows": there, "cols": c} if stage == 0 else {"rows": r, "cols": there}
        return pltpu.make_async_remote_copy(
            src_ref=buf.at[pos], dst_ref=buf.at[there],
            send_sem=ar_ssem.at[stage, k], recv_sem=ar_rsem.at[stage, there],
            device_id=device, device_id_type=MESH,
        )

    for k in range(1, n_rows):
        reduce_copy(0, k).start()

    def pair(k_prob, k_grad, finish):
        def one(bi, carry):
            def channels(i, acc):
                for extra in range(3):
                    ch = 3 * i + extra
                    p_own = shift[k_prob, REACH, ch, rows_at(REACH), :]
                    m_own = shift[k_grad, REACH, ch, rows_at(REACH), :]
                    acc = tuple(
                        acc[a]
                        + m_own * shift[k_prob, bi, ch, rows_at(a), :]
                        + shift[k_grad, bi, ch, rows_at(a), :] * p_own
                        for a in range(SPAN)
                    )
                return acc

            zero = jnp.zeros((height, LANES), f32)
            acc = lax.fori_loop(0, classes // 3, channels, (zero,) * SPAN)
            for a in range(SPAN):
                finish(bi * SPAN + a, acc[a])
            return carry

        lax.fori_loop(0, SPAN, one, 0)

    def keep(o, value):
        coef[o] = value

    def close(o, value):
        coef[o] = (coef[o] + value) * kern[o] * (1.0 / feats)

    pair(1, 2, keep)

    for k in range(1, n_rows):
        reduce_arrival(0, k).wait_recv()
    ar_two[c] = jnp.sum(ar_one[...], axis=0)
    for k in range(1, n_cols):
        reduce_copy(1, k).start()

    arrive(3)
    spread_out(3, ug_ref)
    ug_ref[...] = lgrad[1] + lgrad[0] + softmax_grad(prob[0], ug_ref[...])
    pair(0, 3, close)

    def feature_block(i, carry):
        base = 4 * i
        chans = pl.ds(base, 4)
        center = f_shift[REACH, chans, rows_at(REACH), :]

        def step(bi, acc):
            for a in range(SPAN):
                acc = acc + coef[bi * SPAN + a][None] * (f_shift[bi, chans, rows_at(a), :] - center)
            return acc

        fg_ref[chans] = lax.fori_loop(0, SPAN, step, jnp.zeros((4, height, LANES), f32))
        return carry

    lax.fori_loop(0, feats // 4, feature_block, 0)

    for k in range(1, n_cols):
        reduce_arrival(1, k).wait_recv()
    cg_ref[...] = jnp.sum(ar_two[...], axis=0)[0:classes, 0:classes]

    each_way(feature_copy, "send")
    for k in range(PHASES):
        each_way(functools.partial(field_copy, k), "send")
    for stage, size in ((0, n_rows), (1, n_cols)):
        for k in range(1, size):
            reduce_copy(stage, k).wait_send()


def on_device(n_rows, n_cols, unary, features, compat, grad_output):
    classes, height, width = unary.shape
    feats = features.shape[0]
    f32 = jnp.float32
    vmem, dma = pltpu.VMEM, pltpu.SemaphoreType.DMA
    groups = feats // F_GROUP
    any_spec = pl.BlockSpec(memory_space=pl.ANY)
    vmem_spec = pl.BlockSpec(memory_space=pltpu.VMEM)
    return pl.pallas_call(
        functools.partial(kernel, n_rows, n_cols, classes, feats),
        out_shape=(
            jax.ShapeDtypeStruct((classes, height, width), f32),
            jax.ShapeDtypeStruct((feats, height, width), f32),
            jax.ShapeDtypeStruct((classes, classes), f32),
        ),
        in_specs=[any_spec, any_spec, pl.BlockSpec(memory_space=pltpu.SMEM), any_spec],
        out_specs=(vmem_spec, vmem_spec, vmem_spec),
        scratch_shapes=[
            vmem((classes, height, width), f32),
            vmem((classes, height, width), f32),
            vmem((feats, height, width), features.dtype),
            vmem((feats, PLANE, width), f32),
            vmem((classes, PLANE, width), f32),
            vmem((SPAN, feats, WIN, width), f32),
            vmem((PHASES, SPAN, classes, WIN, width), f32),
            vmem((SPAN * SPAN, height, width), f32),
            vmem((SPAN * SPAN, height, width), f32),
            vmem((PHASES, classes, height, width), f32),
            vmem((2, classes, height, width), f32),
            vmem((2, classes, height, width), f32),
            vmem((3 * feats, width), f32),
            vmem((2, 3 * feats, width), jnp.bfloat16),
            vmem((2, 3 * feats, width), jnp.bfloat16),
            vmem((groups, height, width), jnp.bfloat16),
            vmem((2, 3, groups, height, width), jnp.bfloat16),
            vmem((groups, 3 * height, width), f32),
            vmem((PHASES, 2, 64, width), f32),
            vmem((PHASES, 2, 64, width), f32),
            vmem((PHASES, height, width), f32),
            vmem((PHASES, 2, PLANE, width), f32),
            vmem((n_rows, 24, width), f32),
            vmem((n_cols, 24, width), f32),
            dma((3,)), dma((8,)), dma((8,)), dma((PHASES, 8)), dma((PHASES, 8)),
            dma((2, max(n_rows, n_cols))), dma((2, max(n_rows, n_cols))),
        ],
        compiler_params=pltpu.CompilerParams(collective_id=0, has_side_effects=True, vmem_limit_bytes=60 * 1024 * 1024),
        name="crf_backward",
    )(unary, features, compat, grad_output)


def solution(mesh):
    placed = (P(None, "rows", "cols"), P(None, "rows", "cols"), P(), P(None, "rows", "cols"))
    return jax.shard_map(
        functools.partial(on_device, mesh.shape["rows"], mesh.shape["cols"]),
        mesh=mesh,
        in_specs=placed,
        out_specs=(P(None, "rows", "cols"), P(None, "rows", "cols"), P()),
        check_vma=False,
    )
```

```python
import functools
import math

import jax
import jax.numpy as jnp
from jax import lax
from jax.experimental import pallas as pl
from jax.experimental.pallas import tpu as pltpu
from jax.sharding import PartitionSpec as P

REACH = 3
SPAN = 2 * REACH + 1
THETA_PIXELS = 3.0
MESH = pl.DeviceIdType.MESH
LANES = 128
TOP = 8
PLANE = 32
WIN = 24
F_GROUP = 16
PHASES = 4
HALF = 8

ROUTES = (
    (-1, 0, 1),
    (1, 0, 0),
    (0, -1, 3),
    (0, 1, 2),
    (-1, -1, 7),
    (-1, 1, 5),
    (1, -1, 6),
    (1, 1, 4),
)


def kernel(
    n_rows, n_cols, classes, feats,
    u_hbm, f_hbm, cm, g_hbm,
    ug_ref, fg_ref, cg_ref,
    u_v, g_v, f_v, f_plane, plane, f_shift, shift, kern, coef,
    prob, msg, lgrad,
    f_rows_f32, f_srow, f_rrow, f_sstrip, f_rstrip, f_strip,
    srow, rrow, sstrip, rstrip,
    ar_one, ar_two,
    in_sem, f_ssem, f_rsem, ssem, rsem, ar_ssem, ar_rsem,
):
    f32 = jnp.float32
    height = u_v.shape[1]
    r = lax.axis_index("rows")
    c = lax.axis_index("cols")
    lane = lax.broadcasted_iota(jnp.int32, (1, LANES), 1)
    lane_group = lane // 6
    from_left = (lane % 6) < 3

    loads = [
        pltpu.make_async_copy(f_hbm, f_v, in_sem.at[0]),
        pltpu.make_async_copy(u_hbm, u_v, in_sem.at[1]),
        pltpu.make_async_copy(g_hbm, g_v, in_sem.at[2]),
    ]
    for load in loads:
        load.start()

    def inside(dr, dc):
        ok = None
        for pos, step, size in ((r, dr, n_rows), (c, dc, n_cols)):
            if step:
                here = (pos > 0) if step < 0 else (pos < size - 1)
                ok = here if ok is None else jnp.logical_and(ok, here)
        return ok

    def target(dr, dc):
        return {"rows": r + dr, "cols": c + dc}

    @pl.when(r == 0)
    def _():
        f_rrow[0] = jnp.zeros_like(f_rrow[0])
        for k in range(PHASES):
            rrow[k, 0] = jnp.zeros_like(rrow[k, 0])
        for side in range(2):
            f_rstrip[side, 0] = jnp.zeros_like(f_rstrip[side, 0])
            for k in range(PHASES):
                rstrip[k, side, 0:HALF] = jnp.zeros((HALF, LANES), f32)

    @pl.when(r == n_rows - 1)
    def _():
        f_rrow[1] = jnp.zeros_like(f_rrow[1])
        for k in range(PHASES):
            rrow[k, 1] = jnp.zeros_like(rrow[k, 1])
        for side in range(2):
            f_rstrip[side, 2] = jnp.zeros_like(f_rstrip[side, 2])
            for k in range(PHASES):
                rstrip[k, side, PLANE - HALF:PLANE] = jnp.zeros((HALF, LANES), f32)

    for side, edge in ((0, 0), (1, n_cols - 1)):
        @pl.when(c == edge)
        def _(side=side):
            f_rstrip[side] = jnp.zeros_like(f_rstrip[side])
            for k in range(PHASES):
                rstrip[k, side] = jnp.zeros((PLANE, LANES), f32)

    barrier = pltpu.get_barrier_semaphore()
    for k in range(1, n_rows):
        pl.semaphore_signal(barrier, inc=1, device_id={"rows": lax.rem(r + k, n_rows), "cols": c}, device_id_type=MESH)
    for k in range(1, n_cols):
        pl.semaphore_signal(barrier, inc=1, device_id={"rows": r, "cols": lax.rem(c + k, n_cols)}, device_id_type=MESH)
    for dr, dc, _ in ROUTES[4:]:
        there = {"rows": lax.rem(r + dr + n_rows, n_rows), "cols": lax.rem(c + dc + n_cols, n_cols)}
        pl.semaphore_signal(barrier, inc=1, device_id=there, device_id_type=MESH)

    def pack_rows(source, count, base_row, dst):
        for ch in range(count):
            dst[3 * ch:3 * ch + 3, :] = source[ch, base_row:base_row + 3, :]

    loads[0].wait()
    f_plane[:, TOP:TOP + height, :] = f_v[...].astype(f32)
    for side, base_row in ((0, TOP), (1, TOP + height - 3)):
        pack_rows(f_plane, feats, base_row, f_rows_f32)
        f_srow[side] = f_rows_f32[...].astype(jnp.bfloat16)
    for group in range(feats // F_GROUP):
        tile = jnp.zeros((height, LANES), f32)
        for k in range(F_GROUP):
            turned = pltpu.roll(f_plane[group * F_GROUP + k, TOP:TOP + height, :], 6 * k + 3, 1)
            tile = jnp.where(lane_group == k, turned, tile)
        f_sstrip[group] = tile.astype(jnp.bfloat16)

    def softmax(values):
        top = jnp.max(values, axis=0, keepdims=True)
        grown = jnp.exp(values - top)
        return grown / jnp.sum(grown, axis=0, keepdims=True)

    def pack(k, ref):
        plane[:, TOP:TOP + height, :] = ref[...]
        tile = jnp.zeros((height, LANES), f32)
        for ch in range(classes):
            turned = pltpu.roll(ref[ch], (6 * ch + 3) % LANES, 1)
            tile = jnp.where(lane_group == ch, turned, tile)
        sstrip[k] = tile
        pack_rows(plane, classes, TOP, srow.at[k, 0])
        pack_rows(plane, classes, TOP + height - 3, srow.at[k, 1])

    def field_copy(k, way):
        dr, dc, slot = ROUTES[way]
        if dc == 0:
            src = srow.at[k, 0 if dr < 0 else 1]
            dst = rrow.at[k, slot]
        else:
            side = 1 if dc < 0 else 0
            if dr == 0:
                src = sstrip.at[k]
                dst = rstrip.at[k, side, pl.ds(HALF, height)]
            elif dr < 0:
                src = sstrip.at[k, pl.ds(0, HALF)]
                dst = rstrip.at[k, side, pl.ds(HALF + height, HALF)]
            else:
                src = sstrip.at[k, pl.ds(height - HALF, HALF)]
                dst = rstrip.at[k, side, pl.ds(0, HALF)]
        return pltpu.make_async_remote_copy(
            src_ref=src, dst_ref=dst, send_sem=ssem.at[k, way], recv_sem=rsem.at[k, way],
            device_id=target(dr, dc), device_id_type=MESH,
        )

    def feature_copy(way):
        dr, dc, slot = ROUTES[way]
        if dc == 0:
            src = f_srow.at[0 if dr < 0 else 1]
            dst = f_rrow.at[slot]
        else:
            src = f_sstrip
            dst = f_rstrip.at[1 if dc < 0 else 0, 1 - dr]
        return pltpu.make_async_remote_copy(
            src_ref=src, dst_ref=dst, send_sem=f_ssem.at[way], recv_sem=f_rsem.at[way],
            device_id=target(dr, dc), device_id_type=MESH,
        )

    def each_way(make, act):
        for way, (dr, dc, _) in enumerate(ROUTES):
            if act == "start":
                @pl.when(inside(dr, dc))
                def _(way=way):
                    make(way).start()
            elif act == "recv":
                @pl.when(inside(-dr, -dc))
                def _(way=way):
                    make(way).wait_recv()
            else:
                @pl.when(inside(dr, dc))
                def _(way=way):
                    make(way).wait_send()

    loads[1].wait()
    prob[0] = softmax(u_v[...])
    pack(0, prob.at[0])
    loads[2].wait()
    pl.semaphore_wait(barrier, n_rows - 1 + n_cols - 1 + 4)
    each_way(feature_copy, "start")
    each_way(functools.partial(field_copy, 0), "start")

    def turn(edge, own, dst, ch):
        for b in range(-REACH, REACH + 1):
            if b == 0:
                dst[b + REACH, ch] = own
            elif b > 0:
                dst[b + REACH, ch] = pltpu.roll(jnp.where(lane < b, edge, own), LANES - b, 1)
            else:
                dst[b + REACH, ch] = pltpu.roll(jnp.where(lane >= LANES + b, edge, own), -b, 1)

    each_way(feature_copy, "recv")
    for side, base_row in ((0, TOP - 3), (1, TOP + height)):
        f_rows_f32[...] = f_rrow[side].astype(f32)
        for ch in range(feats):
            f_plane[ch, base_row:base_row + 3, :] = f_rows_f32[3 * ch:3 * ch + 3, :]
    for group in range(feats // F_GROUP):
        for part in range(3):
            both = jnp.where(
                from_left, f_rstrip[0, part, group].astype(f32), f_rstrip[1, part, group].astype(f32)
            )
            f_strip[group, part * height:(part + 1) * height] = both
    for group in range(feats // F_GROUP):
        strip = f_strip[group, height - 3:height - 3 + WIN]

        def f_turn(i, carry, group=group, strip=strip):
            for extra in range(8):
                k = 8 * i + extra
                ch = group * F_GROUP + k
                edge = pltpu.roll(strip, LANES - 3 - 6 * k, 1)
                turn(edge, f_plane[ch, TOP - 3:TOP - 3 + WIN, :], f_shift, ch)
            return carry

        lax.fori_loop(0, F_GROUP // 8, f_turn, 0)

    factor = 1.0 / (2.0 * feats)
    spread = 1.0 / (2.0 * THETA_PIXELS * THETA_PIXELS)

    def rows_at(a):
        return slice(a, a + height)

    def affinity(bi, carry):
        def channels(i, acc):
            for extra in range(8):
                ch = 8 * i + extra
                center = f_shift[REACH, ch, rows_at(REACH), :]
                new = []
                for a in range(SPAN):
                    gap = f_shift[bi, ch, rows_at(a), :] - center
                    new.append(acc[a] + gap * gap)
                acc = tuple(new)
            return acc

        zero = jnp.zeros((height, LANES), f32)
        acc = lax.fori_loop(0, feats // 8, channels, (zero,) * SPAN)
        step = (bi - REACH).astype(f32)
        for a in range(SPAN):
            away = ((a - REACH) * (a - REACH) + step * step) * spread
            kern[bi * SPAN + a] = jnp.exp(-acc[a] * factor - away)
        return carry

    lax.fori_loop(0, SPAN, affinity, 0)
    kern[REACH * SPAN + REACH] = jnp.zeros((height, LANES), f32)

    def arrive(k):
        each_way(functools.partial(field_copy, k), "recv")
        for ch in range(classes):
            plane[ch, TOP - 3:TOP, :] = rrow[k, 0, 3 * ch:3 * ch + 3, :]
            plane[ch, TOP + height:TOP + height + 3, :] = rrow[k, 1, 3 * ch:3 * ch + 3, :]
        strip = jnp.where(from_left, rstrip[k, 0, TOP - 3:TOP - 3 + WIN], rstrip[k, 1, TOP - 3:TOP - 3 + WIN])

        def f_turn(i, carry):
            for extra in range(7):
                ch = 7 * i + extra
                edge = pltpu.roll(strip, LANES - 3 - 6 * ch, 1)
                turn(edge, plane[ch, TOP - 3:TOP - 3 + WIN, :], shift.at[k], ch)
            return carry

        lax.fori_loop(0, classes // 7, f_turn, 0)

    def spread_out(k, dst):
        for block in range(classes // 7):
            chans = slice(7 * block, 7 * block + 7)

            def step(bi, acc):
                for a in range(SPAN):
                    acc = acc + kern[bi * SPAN + a][None] * shift[k, bi, chans, rows_at(a), :]
                return acc

            dst[chans] = lax.fori_loop(0, SPAN, step, jnp.zeros((7, height, LANES), f32))

    def mix(transposed, source, finish):
        def block(i, carry):
            acc = [jnp.zeros((height, LANES), f32)] * 7
            for d in range(classes):
                value = source[d]
                for j in range(7):
                    ch = 7 * i + j
                    weight = cm[d, ch] if transposed else cm[ch, d]
                    acc[j] = acc[j] + weight * value
            for j in range(7):
                finish(7 * i + j, acc[j])
            return carry

        lax.fori_loop(0, classes // 7, block, 0)

    def set_logits(t):
        def finish(ch, acc):
            prob[t, ch] = u_v[ch] - acc
        return finish

    def set_msg_grad(ch, acc):
        plane[ch, TOP:TOP + height, :] = -acc
        prob[PHASES - 1, ch] = -acc

    def softmax_grad(value, cotangent):
        return value * (cotangent - jnp.sum(cotangent * value, axis=0, keepdims=True))

    arrive(0)
    spread_out(0, msg.at[0])
    mix(False, msg.at[0], set_logits(1))
    prob[1] = softmax(prob[1])
    pack(1, prob.at[1])
    each_way(functools.partial(field_copy, 1), "start")
    arrive(1)
    spread_out(1, msg.at[1])
    mix(False, msg.at[1], set_logits(2))
    prob[2] = softmax(prob[2])

    lgrad[1] = softmax_grad(prob[2], g_v[...])
    mix(True, lgrad.at[1], set_msg_grad)
    pack(2, prob.at[PHASES - 1])
    each_way(functools.partial(field_copy, 2), "start")

    def by_pixel(ref):
        return jnp.concatenate([ref[:, y, :] for y in range(height)], axis=1)

    def outer(t):
        return lax.dot_general(
            by_pixel(lgrad.at[t]), by_pixel(msg.at[t]), (((1,), (1,)), ((), ())),
            precision=lax.Precision.HIGHEST, preferred_element_type=f32,
        )

    total = outer(1)
    arrive(2)
    spread_out(2, ug_ref)

    lgrad[0] = softmax_grad(prob[1], ug_ref[...])
    mix(True, lgrad.at[0], set_msg_grad)
    pack(3, prob.at[PHASES - 1])
    each_way(functools.partial(field_copy, 3), "start")

    pixels = height * n_rows * LANES * n_cols
    total = (total + outer(0)) * (-1.0 / math.sqrt(pixels))
    ar_one[r, 0:classes, 0:classes] = total

    def reduce_copy(stage, k):
        buf = (ar_one, ar_two)[stage]
        size, pos = ((n_rows, r), (n_cols, c))[stage]
        there = lax.rem(pos + k, size)
        device = {"rows": there, "cols": c} if stage == 0 else {"rows": r, "cols": there}
        return pltpu.make_async_remote_copy(
            src_ref=buf.at[pos], dst_ref=buf.at[pos],
            send_sem=ar_ssem.at[stage, k], recv_sem=ar_rsem.at[stage, pos],
            device_id=device, device_id_type=MESH,
        )

    def reduce_arrival(stage, k):
        buf = (ar_one, ar_two)[stage]
        size, pos = ((n_rows, r), (n_cols, c))[stage]
        there = lax.rem(pos + k, size)
        device = {"rows": there, "cols": c} if stage == 0 else {"rows": r, "cols": there}
        return pltpu.make_async_remote_copy(
            src_ref=buf.at[pos], dst_ref=buf.at[there],
            send_sem=ar_ssem.at[stage, k], recv_sem=ar_rsem.at[stage, there],
            device_id=device, device_id_type=MESH,
        )

    for k in range(1, n_rows):
        reduce_copy(0, k).start()

    def pair(k_prob, k_grad, finish):
        def one(bi, carry):
            def channels(i, acc):
                for extra in range(7):
                    ch = 7 * i + extra
                    p_own = shift[k_prob, REACH, ch, rows_at(REACH), :]
                    m_own = shift[k_grad, REACH, ch, rows_at(REACH), :]
                    acc = tuple(
                        acc[a]
                        + m_own * shift[k_prob, bi, ch, rows_at(a), :]
                        + shift[k_grad, bi, ch, rows_at(a), :] * p_own
                        for a in range(SPAN)
                    )
                return acc

            zero = jnp.zeros((height, LANES), f32)
            acc = lax.fori_loop(0, classes // 7, channels, (zero,) * SPAN)
            for a in range(SPAN):
                finish(bi * SPAN + a, acc[a])
            return carry

        lax.fori_loop(0, SPAN, one, 0)

    def keep(o, value):
        coef[o] = value

    def close(o, value):
        coef[o] = (coef[o] + value) * kern[o] * (1.0 / feats)

    pair(1, 2, keep)

    for k in range(1, n_rows):
        reduce_arrival(0, k).wait_recv()
    ar_two[c] = jnp.sum(ar_one[...], axis=0)
    for k in range(1, n_cols):
        reduce_copy(1, k).start()

    arrive(3)
    spread_out(3, ug_ref)
    ug_ref[...] = lgrad[1] + lgrad[0] + softmax_grad(prob[0], ug_ref[...])
    pair(0, 3, close)

    weight_sum = jnp.sum(coef[...], axis=0)

    def feature_block(i, carry):
        chans = pl.ds(8 * i, 8)

        def step(bi, acc):
            for a in range(SPAN):
                acc = acc + coef[bi * SPAN + a][None] * f_shift[bi, chans, rows_at(a), :]
            return acc

        start = -weight_sum[None] * f_shift[REACH, chans, rows_at(REACH), :]
        fg_ref[chans] = lax.fori_loop(0, SPAN, step, start)
        return carry

    lax.fori_loop(0, feats // 8, feature_block, 0)

    for k in range(1, n_cols):
        reduce_arrival(1, k).wait_recv()
    cg_ref[...] = jnp.sum(ar_two[...], axis=0)[0:classes, 0:classes]

    each_way(feature_copy, "send")
    for k in range(PHASES):
        each_way(functools.partial(field_copy, k), "send")
    for stage, size in ((0, n_rows), (1, n_cols)):
        for k in range(1, size):
            reduce_copy(stage, k).wait_send()


def on_device(n_rows, n_cols, unary, features, compat, grad_output):
    classes, height, width = unary.shape
    feats = features.shape[0]
    f32 = jnp.float32
    vmem, dma = pltpu.VMEM, pltpu.SemaphoreType.DMA
    groups = feats // F_GROUP
    any_spec = pl.BlockSpec(memory_space=pl.ANY)
    vmem_spec = pl.BlockSpec(memory_space=pltpu.VMEM)
    return pl.pallas_call(
        functools.partial(kernel, n_rows, n_cols, classes, feats),
        out_shape=(
            jax.ShapeDtypeStruct((classes, height, width), f32),
            jax.ShapeDtypeStruct((feats, height, width), f32),
            jax.ShapeDtypeStruct((classes, classes), f32),
        ),
        in_specs=[any_spec, any_spec, pl.BlockSpec(memory_space=pltpu.SMEM), any_spec],
        out_specs=(vmem_spec, vmem_spec, vmem_spec),
        scratch_shapes=[
            vmem((classes, height, width), f32),
            vmem((classes, height, width), f32),
            vmem((feats, height, width), features.dtype),
            vmem((feats, PLANE, width), f32),
            vmem((classes, PLANE, width), f32),
            vmem((SPAN, feats, WIN, width), f32),
            vmem((PHASES, SPAN, classes, WIN, width), f32),
            vmem((SPAN * SPAN, height, width), f32),
            vmem((SPAN * SPAN, height, width), f32),
            vmem((PHASES, classes, height, width), f32),
            vmem((2, classes, height, width), f32),
            vmem((2, classes, height, width), f32),
            vmem((3 * feats, width), f32),
            vmem((2, 3 * feats, width), jnp.bfloat16),
            vmem((2, 3 * feats, width), jnp.bfloat16),
            vmem((groups, height, width), jnp.bfloat16),
            vmem((2, 3, groups, height, width), jnp.bfloat16),
            vmem((groups, 3 * height, width), f32),
            vmem((PHASES, 2, 64, width), f32),
            vmem((PHASES, 2, 64, width), f32),
            vmem((PHASES, height, width), f32),
            vmem((PHASES, 2, PLANE, width), f32),
            vmem((n_rows, 24, width), f32),
            vmem((n_cols, 24, width), f32),
            dma((3,)), dma((8,)), dma((8,)), dma((PHASES, 8)), dma((PHASES, 8)),
            dma((2, max(n_rows, n_cols))), dma((2, max(n_rows, n_cols))),
        ],
        compiler_params=pltpu.CompilerParams(collective_id=0, has_side_effects=True, vmem_limit_bytes=60 * 1024 * 1024),
        name="crf_backward",
    )(unary, features, compat, grad_output)


def solution(mesh):
    placed = (P(None, "rows", "cols"), P(None, "rows", "cols"), P(), P(None, "rows", "cols"))
    return jax.shard_map(
        functools.partial(on_device, mesh.shape["rows"], mesh.shape["cols"]),
        mesh=mesh,
        in_specs=placed,
        out_specs=(P(None, "rows", "cols"), P(None, "rows", "cols"), P()),
        check_vma=False,
    )
```
